32 devices in a mesh: layer: 2 (over x), row: 4 (over y, core), col: 4 (over z).
Axes of the slice: x: 2, y: 2, z: 4, core: 2. Of those that a mesh axis runs over, the one named last changes fastest.
Arguments:
- down_source: float32 [2, 64, 4096], P('layer', None, ('row', 'col')), may hold values from -3 to 3
- up_source: float32 [2, 64, 4096], P('layer', None, ('row', 'col')), may hold values from -3 to 3
- down_transfer: bfloat16 [2, 4096, 4, 1024], P('layer', 'row', None, 'col'), may hold values from -0.09375 to 0.09375
- up_transfer: bfloat16 [2, 4096, 4, 1024], P('layer', 'row', None, 'col'), may hold values from -0.09375 to 0.09375
- reflection: bfloat16 [2, 4096, 4, 1024], P('layer', 'row', None, 'col'), may hold values from -0.09375 to 0.09375
Outputs:
- traces: float32 [2, 64, 4096], P('layer', None, ('row', 'col'))
The draws below stay inside these ranges and needn't reach their ends.
All inputs are finite; a program needn't handle non-finite values.
Results may differ from the reference program's by a relative error of at most 0.015.
Values may be sent and summed in bfloat16 or wider, within the bound.
A program may use at most 64 MiB of HBM per device.

```python
import jax
import jax.numpy as jnp
from jax import lax

W = 4096
S = 64
LAYERS = 2
BLOCKS = 4
PIECE = 1024


def levels(stream_key, extent, shards, smallest, top_value):
    def one(dim, blocks):
        heights = jax.random.uniform(jax.random.fold_in(jax.random.fold_in(stream_key, 6), dim), (blocks,), jnp.float32, smallest / len(shards), top_value / len(shards))
        return jnp.repeat(jnp.exp(heights), extent[dim] // blocks).reshape((-1,) + (1,) * (len(extent) - dim - 1))

    loudness = one(*shards[0])
    for cut in shards[1:]:
        loudness = loudness * one(*cut)
    return loudness


def scatter_about(key, dims, spread, reach, pieces=(), kind=jnp.bfloat16):
    array = jax.random.normal(key, dims, jnp.float32) * spread
    if len(pieces) > 0:
        array = levels(key, dims, pieces, -0.22, 0.18) * array
    return jnp.clip(array, min=-reach, max=reach).astype(kind)


def setup_inputs(seed: int = 0) -> dict:
    key_of = jax.random.split(jax.random.key(seed), 6)
    down_source = scatter_about(key_of[0], (LAYERS, S, W), 0.5, 3.0, ((0, 2), (2, 16)), jnp.float32)
    up_source = scatter_about(key_of[1], (LAYERS, S, W), 0.5, 3.0, ((0, 2), (2, 16)), jnp.float32)
    down_transfer = scatter_about(key_of[2], (LAYERS, W, BLOCKS, PIECE), W ** -0.5, 0.09375, ((0, 2), (1, 4), (3, 4)))
    up_transfer = scatter_about(key_of[3], (LAYERS, W, BLOCKS, PIECE), W ** -0.5, 0.09375, ((0, 2), (1, 4), (3, 4)))
    reflection = scatter_about(key_of[4], (LAYERS, W, BLOCKS, PIECE), W ** -0.5, 0.09375, ((0, 2), (1, 4), (3, 4)))
    return dict(down_source=down_source, up_source=up_source, down_transfer=down_transfer, up_transfer=up_transfer, reflection=reflection)


def reference(down_source, up_source, down_transfer, up_transfer, reflection):
    count = down_source.shape[0]
    width = down_source.shape[2]
    down_ops = down_transfer.reshape(count, width, width)
    up_ops = up_transfer.reshape(count, width, width)
    reflect_ops = reflection.reshape(count, width, width)
    zero_trace = jnp.zeros((down_source.shape[1], width), jnp.bfloat16)

    def advance(previous, inputs):
        source_now, operator = inputs
        current = source_now + jnp.dot(previous, operator.T, preferred_element_type=jnp.float32)
        return current.astype(jnp.bfloat16), current

    unused_down, down = lax.scan(advance, zero_trace, (down_source, down_ops))
    unused_up, up = lax.scan(advance, zero_trace, (up_source, up_ops), reverse=True)
    mixed_trace = (down + up).astype(jnp.bfloat16)

    def reflect_one(inputs):
        trace_now, operator = inputs
        return jnp.dot(trace_now, operator.T, preferred_element_type=jnp.float32)

    reflected = lax.map(reflect_one, (mixed_trace, reflect_ops))
    return down + up + reflected
```

```python
import functools

import jax
import jax.numpy as jnp
from jax import lax
from jax.experimental import pallas as pl
from jax.experimental.pallas import tpu as pltpu
from jax.sharding import PartitionSpec as P

PARTS = 1
MESH = pl.DeviceIdType.MESH


def passed_along(block, axis, distance):
    devices = range(lax.axis_size(axis))
    route = [(i - distance, i) for i in devices if i - distance in devices]
    return lax.ppermute(block, axis, route)


def contract(data_rows, matrix_rows):
    return lax.dot_general(
        data_rows, matrix_rows, (((1,), (1,)), ((), ())), preferred_element_type=jnp.float32
    )


def early_rounds(own_down, own_up, down_transfer, up_transfer, rounds):
    height = down_transfer.shape[1]
    down_tile = down_transfer[0].reshape(height, -1)
    up_tile = up_transfer[0].reshape(height, -1)

    def gain(trace, distance, tile):
        moved = passed_along(trace.astype(jnp.bfloat16), "layer", distance)
        pieces = lax.all_gather(moved, "row", axis=1, tiled=True)
        return lax.psum_scatter(contract(pieces, tile), "col", scatter_dimension=1, tiled=True)

    def one(counter, carried):
        down_now, up_now = carried
        return own_down + gain(down_now, 1, down_tile), own_up + gain(up_now, -1, up_tile)

    return lax.fori_loop(0, rounds, one, (own_down, own_up))


def kernel(
    layers, rows, cols,
    down_ref, up_ref, wdown_ref, wup_ref, wreflect_ref, out_ref,
    down_v, up_v, stage_t, stage_r, wide, mat_t, mat_r,
    send_down, send_up, xbuf, part1, rs1, own1, summed, gbuf, part2, rs2, own2,
    load_sem, down_sem, up_sem, x_sem, p1_sem, rs1_sem, g_send_sem, g_sem, p2_sem, rs2_sem,
):
    l, r, c = lax.axis_index("layer"), lax.axis_index("row"), lax.axis_index("col")
    parts, size, width = xbuf.shape[1:]
    groups = stage_t.shape[0] // mat_t.shape[0]
    lane = stage_t.shape[1]

    def dev(layer, row, col):
        return (layer, row, col)

    load_down = pltpu.make_async_copy(down_ref.at[0], down_v, load_sem.at[0])
    load_up = pltpu.make_async_copy(up_ref.at[0], up_v, load_sem.at[1])
    load_down.start()
    load_up.start()
    load_t = pltpu.make_async_copy(wdown_ref, stage_t, load_sem.at[2])
    load_tu = pltpu.make_async_copy(wup_ref, stage_t, load_sem.at[2])
    load_r = pltpu.make_async_copy(wreflect_ref, stage_r, load_sem.at[3])

    @pl.when(l == 0)
    def _():
        load_tu.start()

    @pl.when(l == layers - 1)
    def _():
        load_t.start()

    load_r.start()

    barrier = pltpu.get_barrier_semaphore()

    def greet(layer, row, col):
        pl.semaphore_signal(barrier, inc=1, device_id=dev(layer, row, col), device_id_type=MESH)

    for d in range(1, cols):
        greet(l, r, lax.rem(c + d, cols))
    for d in range(1, rows):
        greet(l, lax.rem(r + d, rows), c)
    if layers == 2:
        for d in range(rows):
            greet(1 - l, lax.rem(r + d, rows), c)
        neighbours = 1
    else:
        @pl.when(l > 0)
        def _():
            for d in range(rows):
                greet(l - 1, lax.rem(r + d, rows), c)

        @pl.when(l < layers - 1)
        def _():
            for d in range(rows):
                greet(l + 1, lax.rem(r + d, rows), c)

        neighbours = jnp.where(l > 0, 1, 0) + jnp.where(l < layers - 1, 1, 0)

    load_down.wait()
    load_up.wait()
    for h in range(parts):
        send_down[h] = down_v[h * size:(h + 1) * size].astype(jnp.bfloat16)
        send_up[h] = up_v[h * size:(h + 1) * size].astype(jnp.bfloat16)
    pl.semaphore_wait(barrier, rows * neighbours + (rows - 1) + (cols - 1))

    order = sorted(range(rows), key=lambda d: (abs(d - rows // 2), -d))

    def source_copies(buffer, sems, layer):
        return [
            pltpu.make_async_remote_copy(
                src_ref=buffer.at[h],
                dst_ref=xbuf.at[r, h],
                send_sem=sems.at[h, d],
                recv_sem=x_sem.at[r, h],
                device_id=dev(layer, lax.rem(r + d, rows), c),
                device_id_type=MESH,
            )
            for h in range(parts)
            for d in order
        ]

    @pl.when(l == layers - 2)
    def _():
        for copy in source_copies(send_down, down_sem, l + 1):
            copy.start()

    @pl.when(l == 1)
    def _():
        for copy in source_copies(send_up, up_sem, l - 1):
            copy.start()

    def relayout(stage, mat):
        step = wide.shape[0] // groups

        def one(i, carry):
            wide[...] = stage[pl.ds(pl.multiple_of(i * step * groups, 128), step * groups), :].astype(jnp.float32)
            blocks = groups * lane // width
            for g in range(groups):
                half, b = divmod(g, blocks)
                column = b * width + half * lane
                mat[pl.ds(pl.multiple_of(i * step, 128), step), column:column + lane] = wide[
                    pl.ds(g, step, stride=groups), :
                ].astype(jnp.bfloat16)
            return carry

        lax.fori_loop(0, mat.shape[0] // step, one, 0)

    def far_first(i):
        low = 2 * c < cols - 1
        down_t = cols - 1 - i
        down_t = jnp.where(down_t <= c, down_t - 1, down_t)
        up_t = jnp.where(c <= i, i + 1, i)
        return jnp.where(low, down_t, up_t)

    def product(source, h, mat, target):
        begin = pl.multiple_of(target * width, 128)
        total = None
        for b in range(rows):
            term = contract(source[b, h], mat[pl.ds(begin, width), b * width:(b + 1) * width])
            total = term if total is None else total + term
        return total

    def scatter_copy(h, i, part, sems, landing, landing_sem):
        return pltpu.make_async_remote_copy(
            src_ref=part.at[h, i],
            dst_ref=landing.at[c, h],
            send_sem=sems.at[h, i],
            recv_sem=landing_sem.at[c, h],
            device_id=dev(l, r, far_first(i)),
            device_id_type=MESH,
        )

    def scatter(source, h, mat, part, sems, landing, landing_sem, own):
        for i in range(cols - 1):
            part[h, i] = product(source, h, mat, far_first(i)).astype(jnp.bfloat16)
            scatter_copy(h, i, part, sems, landing, landing_sem).start()
        own[h] = product(source, h, mat, c)

    def arrived(landing, landing_sem, index, h, part):
        pltpu.make_async_remote_copy(
            src_ref=landing.at[index, h],
            dst_ref=landing.at[index, h],
            send_sem=p1_sem.at[0, 0],
            recv_sem=landing_sem.at[index, h],
            device_id=dev(l, r, lax.rem(c + 1, cols)),
            device_id_type=MESH,
        ).wait_recv()

    def collected(h, own, landing, landing_sem):
        total = own[h]
        for d in range(1, cols):
            sender = lax.rem(c + d, cols)
            arrived(landing, landing_sem, sender, h, None)
            total = total + landing[sender, h].astype(jnp.float32)
        return total

    def receives(body):
        if layers == 2:
            body()
        else:
            pl.when((l == 0) | (l == layers - 1))(body)

    @receives
    def _():
        load_t.wait()
        relayout(stage_t, mat_t)
        for h in range(parts):
            for b in range(rows):
                arrived(xbuf, x_sem, b, h, None)
            scatter(xbuf, h, mat_t, part1, p1_sem, rs1, rs1_sem, own1)

    load_r.wait()
    relayout(stage_r, mat_r)

    def gather_copy(h, d):
        return pltpu.make_async_remote_copy(
            src_ref=gbuf.at[r, h],
            dst_ref=gbuf.at[r, h],
            send_sem=g_send_sem.at[h, d],
            recv_sem=g_sem.at[r, h],
            device_id=dev(l, lax.rem(r + d, rows), c),
            device_id_type=MESH,
        )

    gather_order = [d for d in order if d > 0]
    for h in range(parts):
        summed[h] = down_v[h * size:(h + 1) * size] + up_v[h * size:(h + 1) * size]

        @receives
        def _():
            summed[h] = summed[h] + collected(h, own1, rs1, rs1_sem)

        gbuf[r, h] = summed[h].astype(jnp.bfloat16)
        for d in gather_order:
            gather_copy(h, d).start()

    for h in range(parts):
        for d in range(1, rows):
            arrived(gbuf, g_sem, lax.rem(r + d, rows), h, None)
        scatter(gbuf, h, mat_r, part2, p2_sem, rs2, rs2_sem, own2)

    for h in range(parts):
        out_ref[0, h * size:(h + 1) * size] = summed[h] + collected(h, own2, rs2, rs2_sem)

    @pl.when(l == layers - 2)
    def _():
        for copy in source_copies(send_down, down_sem, l + 1):
            copy.wait_send()

    @pl.when(l == 1)
    def _():
        for copy in source_copies(send_up, up_sem, l - 1):
            copy.wait_send()

    for h in range(parts):
        for i in range(cols - 1):
            @receives
            def _():
                scatter_copy(h, i, part1, p1_sem, rs1, rs1_sem).wait_send()

            scatter_copy(h, i, part2, p2_sem, rs2, rs2_sem).wait_send()
        for d in gather_order:
            gather_copy(h, d).wait_send()


def on_device(down_source, up_source, down_transfer, up_transfer, reflection):
    layers, rows, cols = (lax.axis_size(a) for a in ("layer", "row", "col"))
    own_down, own_up = down_source, up_source
    if layers > 2:
        layer = lax.axis_index("layer")
        down_now, up_now = early_rounds(
            own_down[0], own_up[0], down_transfer, up_transfer, layers - 2
        )
        own_down = jnp.where(layer == layers - 1, own_down, down_now[None])
        own_up = jnp.where(layer == 0, own_up, up_now[None])

    _, sources, width = down_source.shape
    _, height, blocks, piece = down_transfer.shape
    lane = 128
    halves = piece // lane
    groups = halves * blocks

    def tiles(w):
        return w.reshape(height, blocks, halves, lane).transpose(0, 2, 1, 3).reshape(-1, lane)

    parts = PARTS
    size = sources // parts
    any_space = pl.BlockSpec(memory_space=pl.ANY)
    vmem = pltpu.VMEM
    f32, bf16 = jnp.float32, jnp.bfloat16
    dma = pltpu.SemaphoreType.DMA
    step = min(height, 256)
    return pl.pallas_call(
        functools.partial(kernel, layers, rows, cols),
        out_shape=jax.ShapeDtypeStruct(down_source.shape, f32),
        in_specs=[any_space] * 5,
        out_specs=pl.BlockSpec(memory_space=pltpu.VMEM),
        scratch_shapes=[
            vmem((sources, width), f32),
            vmem((sources, width), f32),
            vmem((height * groups, lane), bf16),
            vmem((height * groups, lane), bf16),
            vmem((step * groups, lane), f32),
            vmem((height, blocks * piece), bf16),
            vmem((height, blocks * piece), bf16),
            vmem((parts, size, width), bf16),
            vmem((parts, size, width), bf16),
            vmem((rows, parts, size, width), bf16),
            vmem((parts, cols - 1, size, width), bf16),
            vmem((cols, parts, size, width), bf16),
            vmem((parts, size, width), f32),
            vmem((parts, size, width), f32),
            vmem((rows, parts, size, width), bf16),
            vmem((parts, cols - 1, size, width), bf16),
            vmem((cols, parts, size, width), bf16),
            vmem((parts, size, width), f32),
            dma((4,)),
            dma((parts, rows)),
            dma((parts, rows)),
            dma((rows, parts)),
            dma((parts, cols - 1)),
            dma((cols, parts)),
            dma((parts, rows)),
            dma((rows, parts)),
            dma((parts, cols - 1)),
            dma((cols, parts)),
        ],
        compiler_params=pltpu.CompilerParams(collective_id=0, has_side_effects=True),
    )(own_down, own_up, tiles(down_transfer), tiles(up_transfer), tiles(reflection))


def solution(mesh):
    in_specs = (
        P("layer", None, ("row", "col")),
        P("layer", None, ("row", "col")),
        P("layer", "row", None, "col"),
        P("layer", "row", None, "col"),
        P("layer", "row", None, "col"),
    )
    out_specs = P("layer", None, ("row", "col"))
    return jax.shard_map(
        on_device, mesh=mesh, in_specs=in_specs, out_specs=out_specs, check_vma=False
    )
```

```python
import functools

import jax
import jax.numpy as jnp
from jax import lax
from jax.experimental import pallas as pl
from jax.experimental.pallas import tpu as pltpu
from jax.sharding import PartitionSpec as P

PARTS = 1
MESH = pl.DeviceIdType.MESH


def passed_along(block, axis, distance):
    devices = range(lax.axis_size(axis))
    route = [(i - distance, i) for i in devices if i - distance in devices]
    return lax.ppermute(block, axis, route)


def contract(data_rows, matrix_rows):
    return lax.dot_general(
        data_rows, matrix_rows, (((1,), (1,)), ((), ())), preferred_element_type=jnp.float32
    )


def early_rounds(own_down, own_up, down_transfer, up_transfer, rounds):
    height = down_transfer.shape[1]
    down_tile = down_transfer[0].reshape(height, -1)
    up_tile = up_transfer[0].reshape(height, -1)

    def gain(trace, distance, tile):
        moved = passed_along(trace.astype(jnp.bfloat16), "layer", distance)
        pieces = lax.all_gather(moved, "row", axis=1, tiled=True)
        return lax.psum_scatter(contract(pieces, tile), "col", scatter_dimension=1, tiled=True)

    def one(counter, carried):
        down_now, up_now = carried
        return own_down + gain(down_now, 1, down_tile), own_up + gain(up_now, -1, up_tile)

    return lax.fori_loop(0, rounds, one, (own_down, own_up))


def kernel(
    layers, rows, cols,
    down_ref, up_ref, wdown_ref, wup_ref, wreflect_ref, out_ref,
    down_v, up_v, stage_t, stage_r, wide, mat_t, mat_r,
    send_down, send_up, xbuf, part1, rs1, own1, summed, gbuf, part2, rs2, own2,
    load_sem, down_sem, up_sem, x_sem, p1_sem, rs1_sem, g_send_sem, g_sem, p2_sem, rs2_sem,
):
    l, r, c = lax.axis_index("layer"), lax.axis_index("row"), lax.axis_index("col")
    parts, size, width = xbuf.shape[1:]
    groups = stage_t.shape[0] // mat_t.shape[0]
    lane = stage_t.shape[1]

    def dev(layer, row, col):
        return (layer, row, col)

    load_down = pltpu.make_async_copy(down_ref.at[0], down_v, load_sem.at[0])
    load_up = pltpu.make_async_copy(up_ref.at[0], up_v, load_sem.at[1])
    load_down.start()
    load_up.start()
    load_t = pltpu.make_async_copy(wdown_ref, stage_t, load_sem.at[2])
    load_tu = pltpu.make_async_copy(wup_ref, stage_t, load_sem.at[2])
    load_r = pltpu.make_async_copy(wreflect_ref, stage_r, load_sem.at[3])

    @pl.when(l == 0)
    def _():
        load_tu.start()

    @pl.when(l == layers - 1)
    def _():
        load_t.start()

    load_r.start()

    barrier = pltpu.get_barrier_semaphore()

    def greet(layer, row, col):
        pl.semaphore_signal(barrier, inc=1, device_id=dev(layer, row, col), device_id_type=MESH)

    for d in range(1, cols):
        greet(l, r, lax.rem(c + d, cols))
    for d in range(1, rows):
        greet(l, lax.rem(r + d, rows), c)
    if layers == 2:
        for d in range(rows):
            greet(1 - l, lax.rem(r + d, rows), c)
        neighbours = 1
    else:
        @pl.when(l > 0)
        def _():
            for d in range(rows):
                greet(l - 1, lax.rem(r + d, rows), c)

        @pl.when(l < layers - 1)
        def _():
            for d in range(rows):
                greet(l + 1, lax.rem(r + d, rows), c)

        neighbours = jnp.where(l > 0, 1, 0) + jnp.where(l < layers - 1, 1, 0)

    load_down.wait()
    load_up.wait()
    for h in range(parts):
        send_down[h] = down_v[h * size:(h + 1) * size].astype(jnp.bfloat16)
        send_up[h] = up_v[h * size:(h + 1) * size].astype(jnp.bfloat16)
    pl.semaphore_wait(barrier, rows * neighbours + (rows - 1) + (cols - 1))

    order = sorted(range(rows), key=lambda d: (abs(d - rows // 2), -d))

    def source_copies(buffer, sems, layer):
        return [
            pltpu.make_async_remote_copy(
                src_ref=buffer.at[h],
                dst_ref=xbuf.at[r, h],
                send_sem=sems.at[h, d],
                recv_sem=x_sem.at[r, h],
                device_id=dev(layer, lax.rem(r + d, rows), c),
                device_id_type=MESH,
            )
            for h in range(parts)
            for d in order
        ]

    @pl.when(l == layers - 2)
    def _():
        for copy in source_copies(send_down, down_sem, l + 1):
            copy.start()

    @pl.when(l == 1)
    def _():
        for copy in source_copies(send_up, up_sem, l - 1):
            copy.start()

    def relayout(stage, mat):
        step = wide.shape[0] // groups

        def one(i, carry):
            wide[...] = stage[pl.ds(pl.multiple_of(i * step * groups, 128), step * groups), :].astype(jnp.float32)
            blocks = groups * lane // width
            for g in range(groups):
                half, b = divmod(g, blocks)
                column = b * width + half * lane
                mat[pl.ds(pl.multiple_of(i * step, 128), step), column:column + lane] = wide[
                    pl.ds(g, step, stride=groups), :
                ].astype(jnp.bfloat16)
            return carry

        lax.fori_loop(0, mat.shape[0] // step, one, 0)

    def far_first(i):
        low = 2 * c < cols - 1
        down_t = cols - 1 - i
        down_t = jnp.where(down_t <= c, down_t - 1, down_t)
        up_t = jnp.where(c <= i, i + 1, i)
        return jnp.where(low, down_t, up_t)

    def product(source, h, mat, target):
        begin = pl.multiple_of(target * width, 128)
        total = None
        for b in range(rows):
            term = contract(source[b, h], mat[pl.ds(begin, width), b * width:(b + 1) * width])
            total = term if total is None else total + term
        return total

    def scatter_copy(h, i, part, sems, landing, landing_sem):
        return pltpu.make_async_remote_copy(
            src_ref=part.at[h, i],
            dst_ref=landing.at[c, h],
            send_sem=sems.at[h, i],
            recv_sem=landing_sem.at[c, h],
            device_id=dev(l, r, far_first(i)),
            device_id_type=MESH,
        )

    def scatter(source, h, mat, part, sems, landing, landing_sem, own):
        for i in range(cols - 1):
            part[h, i] = product(source, h, mat, far_first(i)).astype(jnp.bfloat16)
            scatter_copy(h, i, part, sems, landing, landing_sem).start()
        own[h] = product(source, h, mat, c)

    def arrived(landing, landing_sem, index, h, part):
        pltpu.make_async_remote_copy(
            src_ref=landing.at[index, h],
            dst_ref=landing.at[index, h],
            send_sem=p1_sem.at[0, 0],
            recv_sem=landing_sem.at[index, h],
            device_id=dev(l, r, lax.rem(c + 1, cols)),
            device_id_type=MESH,
        ).wait_recv()

    def collected(h, own, landing, landing_sem):
        total = own[h]
        for d in range(1, cols):
            sender = lax.rem(c + d, cols)
            arrived(landing, landing_sem, sender, h, None)
            total = total + landing[sender, h].astype(jnp.float32)
        return total

    def receives(body):
        if layers == 2:
            body()
        else:
            pl.when((l == 0) | (l == layers - 1))(body)

    @receives
    def _():
        load_t.wait()
        relayout(stage_t, mat_t)
        for h in range(parts):
            for b in range(rows):
                arrived(xbuf, x_sem, b, h, None)
            scatter(xbuf, h, mat_t, part1, p1_sem, rs1, rs1_sem, own1)

    load_r.wait()
    relayout(stage_r, mat_r)

    def gather_copy(h, d):
        return pltpu.make_async_remote_copy(
            src_ref=gbuf.at[r, h],
            dst_ref=gbuf.at[r, h],
            send_sem=g_send_sem.at[h, d],
            recv_sem=g_sem.at[r, h],
            device_id=dev(l, lax.rem(r + d, rows), c),
            device_id_type=MESH,
        )

    gather_order = [d for d in order if d > 0]
    for h in range(parts):
        summed[h] = down_v[h * size:(h + 1) * size] + up_v[h * size:(h + 1) * size]

        @receives
        def _():
            summed[h] = summed[h] + collected(h, own1, rs1, rs1_sem)

        gbuf[r, h] = summed[h].astype(jnp.bfloat16)
        for d in gather_order:
            gather_copy(h, d).start()

    for h in range(parts):
        for d in range(1, rows):
            arrived(gbuf, g_sem, lax.rem(r + d, rows), h, None)
        scatter(gbuf, h, mat_r, part2, p2_sem, rs2, rs2_sem, own2)

    for h in range(parts):
        out_ref[0, h * size:(h + 1) * size] = summed[h] + collected(h, own2, rs2, rs2_sem)

    @pl.when(l == layers - 2)
    def _():
        for copy in source_copies(send_down, down_sem, l + 1):
            copy.wait_send()

    @pl.when(l == 1)
    def _():
        for copy in source_copies(send_up, up_sem, l - 1):
            copy.wait_send()

    for h in range(parts):
        for i in range(cols - 1):
            @receives
            def _():
                scatter_copy(h, i, part1, p1_sem, rs1, rs1_sem).wait_send()

            scatter_copy(h, i, part2, p2_sem, rs2, rs2_sem).wait_send()
        for d in gather_order:
            gather_copy(h, d).wait_send()


def on_device(down_source, up_source, down_transfer, up_transfer, reflection):
    layers, rows, cols = (lax.axis_size(a) for a in ("layer", "row", "col"))
    own_down, own_up = down_source, up_source
    if layers > 2:
        layer = lax.axis_index("layer")
        down_now, up_now = early_rounds(
            own_down[0], own_up[0], down_transfer, up_transfer, layers - 2
        )
        own_down = jnp.where(layer == layers - 1, own_down, down_now[None])
        own_up = jnp.where(layer == 0, own_up, up_now[None])

    _, sources, width = down_source.shape
    _, height, blocks, piece = down_transfer.shape
    lane = 128
    halves = piece // lane
    groups = halves * blocks

    def tiles(w):
        return w.reshape(height, blocks, halves, lane).transpose(0, 2, 1, 3).reshape(-1, lane)

    parts = PARTS
    size = sources // parts
    any_space = pl.BlockSpec(memory_space=pl.ANY)
    vmem = pltpu.VMEM
    f32, bf16 = jnp.float32, jnp.bfloat16
    dma = pltpu.SemaphoreType.DMA
    step = min(height, 256)
    return pl.pallas_call(
        functools.partial(kernel, layers, rows, cols),
        out_shape=pltpu.VMEM(down_source.shape, f32),
        in_specs=[any_space] * 5,
        out_specs=pl.BlockSpec(memory_space=pltpu.VMEM),
        scratch_shapes=[
            vmem((sources, width), f32),
            vmem((sources, width), f32),
            vmem((height * groups, lane), bf16),
            vmem((height * groups, lane), bf16),
            vmem((step * groups, lane), f32),
            vmem((height, blocks * piece), bf16),
            vmem((height, blocks * piece), bf16),
            vmem((parts, size, width), bf16),
            vmem((parts, size, width), bf16),
            vmem((rows, parts, size, width), bf16),
            vmem((parts, cols - 1, size, width), bf16),
            vmem((cols, parts, size, width), bf16),
            vmem((parts, size, width), f32),
            vmem((parts, size, width), f32),
            vmem((rows, parts, size, width), bf16),
            vmem((parts, cols - 1, size, width), bf16),
            vmem((cols, parts, size, width), bf16),
            vmem((parts, size, width), f32),
            dma((4,)),
            dma((parts, rows)),
            dma((parts, rows)),
            dma((rows, parts)),
            dma((parts, cols - 1)),
            dma((cols, parts)),
            dma((parts, rows)),
            dma((rows, parts)),
            dma((parts, cols - 1)),
            dma((cols, parts)),
        ],
        compiler_params=pltpu.CompilerParams(collective_id=0, has_side_effects=True),
    )(own_down, own_up, tiles(down_transfer), tiles(up_transfer), tiles(reflection))


def solution(mesh):
    in_specs = (
        P("layer", None, ("row", "col")),
        P("layer", None, ("row", "col")),
        P("layer", "row", None, "col"),
        P("layer", "row", None, "col"),
        P("layer", "row", None, "col"),
    )
    out_specs = P("layer", None, ("row", "col"))
    return jax.shard_map(
        on_device, mesh=mesh, in_specs=in_specs, out_specs=out_specs, check_vma=False
    )
```

```python
import functools

import jax
import jax.numpy as jnp
from jax import lax
from jax.experimental import pallas as pl
from jax.experimental.pallas import tpu as pltpu
from jax.sharding import PartitionSpec as P

PARTS = 1
MESH = pl.DeviceIdType.MESH


def passed_along(block, axis, distance):
    devices = range(lax.axis_size(axis))
    route = [(i - distance, i) for i in devices if i - distance in devices]
    return lax.ppermute(block, axis, route)


def contract(data_rows, matrix_rows):
    return lax.dot_general(
        data_rows, matrix_rows, (((1,), (1,)), ((), ())), preferred_element_type=jnp.float32
    )


def early_rounds(own_down, own_up, down_transfer, up_transfer, rounds):
    height = down_transfer.shape[1]
    down_tile = down_transfer[0].reshape(height, -1)
    up_tile = up_transfer[0].reshape(height, -1)

    def gain(trace, distance, tile):
        moved = passed_along(trace.astype(jnp.bfloat16), "layer", distance)
        pieces = lax.all_gather(moved, "row", axis=1, tiled=True)
        return lax.psum_scatter(contract(pieces, tile), "col", scatter_dimension=1, tiled=True)

    def one(counter, carried):
        down_now, up_now = carried
        return own_down + gain(down_now, 1, down_tile), own_up + gain(up_now, -1, up_tile)

    return lax.fori_loop(0, rounds, one, (own_down, own_up))


def kernel(
    layers, rows, cols,
    down_ref, up_ref, wdown_ref, wup_ref, wreflect_ref, out_ref,
    down_v, up_v, stage_t, stage_r, wide, mat_t, mat_r,
    send_down, send_up, xbuf, part1, rs1, own1, summed, gbuf, part2, rs2, own2,
    load_sem, down_sem, up_sem, x_sem, p1_sem, rs1_sem, g_send_sem, g_sem, p2_sem, rs2_sem,
    relay_sem, far_sem,
):
    l, r, c = lax.axis_index("layer"), lax.axis_index("row"), lax.axis_index("col")
    parts, size, width = xbuf.shape[1:]
    groups = stage_t.shape[0] // mat_t.shape[0]
    lane = stage_t.shape[1]

    def dev(layer, row, col):
        return (layer, row, col)

    order = sorted(range(rows), key=lambda d: (abs(d - rows // 2), -d))
    partner = r + 1 - 2 * lax.rem(r, 2)

    barrier = pltpu.get_barrier_semaphore()

    def greet(layer, row, col):
        pl.semaphore_signal(barrier, inc=1, device_id=dev(layer, row, col), device_id_type=MESH)

    source_order = [d for d in order if d % 2 == 0]
    if layers == 2:
        for d in source_order:
            greet(1 - l, lax.rem(r + d, rows), c)
        neighbours = 1
    else:
        @pl.when(l > 0)
        def _():
            for d in source_order:
                greet(l - 1, lax.rem(r + d, rows), c)

        @pl.when(l < layers - 1)
        def _():
            for d in source_order:
                greet(l + 1, lax.rem(r + d, rows), c)

        neighbours = jnp.where(l > 0, 1, 0) + jnp.where(l < layers - 1, 1, 0)

    @pl.when(c > 0)
    def _():
        greet(l, r, c - 1)

    @pl.when(c < cols - 1)
    def _():
        greet(l, r, c + 1)

    beside = jnp.where(c > 0, 1, 0) + jnp.where(c < cols - 1, 1, 0)
    for d in range(1, rows):
        greet(l, lax.rem(r + d, rows), c)

    load_down = pltpu.make_async_copy(down_ref.at[0], down_v, load_sem.at[0])
    load_up = pltpu.make_async_copy(up_ref.at[0], up_v, load_sem.at[1])
    load_down.start()
    load_up.start()
    load_t = pltpu.make_async_copy(wdown_ref, stage_t, load_sem.at[2])
    load_tu = pltpu.make_async_copy(wup_ref, stage_t, load_sem.at[2])
    load_r = pltpu.make_async_copy(wreflect_ref, stage_r, load_sem.at[3])

    @pl.when(l == 0)
    def _():
        load_tu.start()

    @pl.when(l == layers - 1)
    def _():
        load_t.start()

    load_r.start()

    load_down.wait()
    load_up.wait()
    for h in range(parts):
        send_down[h] = down_v[h * size:(h + 1) * size].astype(jnp.bfloat16)
        send_up[h] = up_v[h * size:(h + 1) * size].astype(jnp.bfloat16)
    pl.semaphore_wait(barrier, len(source_order) * neighbours + (rows - 1) + beside)

    def source_copies(buffer, sems, layer):
        return [
            pltpu.make_async_remote_copy(
                src_ref=buffer.at[h],
                dst_ref=xbuf.at[r, h],
                send_sem=sems.at[h, d],
                recv_sem=x_sem.at[r, h],
                device_id=dev(layer, lax.rem(r + d, rows), c),
                device_id_type=MESH,
            )
            for h in range(parts)
            for d in source_order
        ]

    @pl.when(l == layers - 2)
    def _():
        for copy in source_copies(send_down, down_sem, l + 1):
            copy.start()

    @pl.when(l == 1)
    def _():
        for copy in source_copies(send_up, up_sem, l - 1):
            copy.start()

    def tell(hop, side, col):
        pl.semaphore_signal(
            far_sem.at[side, hop], inc=1, device_id=dev(l, r, col), device_id_type=MESH
        )

    def known(hop):
        for side, sign in ((0, -1), (1, 1)):
            there = (c >= hop) if sign < 0 else (c < cols - hop)
            onward = (c < cols - 1) if sign < 0 else (c > 0)

            if hop > 1:
                @pl.when(there)
                def _():
                    pl.semaphore_wait(far_sem.at[side, hop], 1)

            if hop < cols - 1:
                @pl.when(there & onward)
                def _():
                    tell(hop + 1, side, c - sign)

    for hop in range(1, cols - 1):
        known(hop)

    def relayout(stage, mat):
        step = wide.shape[0] // groups

        def one(i, carry):
            wide[...] = stage[pl.ds(pl.multiple_of(i * step * groups, 128), step * groups), :].astype(jnp.float32)
            blocks = groups * lane // width
            for g in range(groups):
                half, b = divmod(g, blocks)
                column = b * width + half * lane
                mat[pl.ds(pl.multiple_of(i * step, 128), step), column:column + lane] = wide[
                    pl.ds(g, step, stride=groups), :
                ].astype(jnp.bfloat16)
            return carry

        lax.fori_loop(0, mat.shape[0] // step, one, 0)

    def far_first(i):
        low = 2 * c < cols - 1
        down_t = cols - 1 - i
        down_t = jnp.where(down_t <= c, down_t - 1, down_t)
        up_t = jnp.where(c <= i, i + 1, i)
        return jnp.where(low, down_t, up_t)

    def product(source, h, mat, target):
        begin = pl.multiple_of(target * width, 128)
        total = None
        for b in range(rows):
            term = contract(source[b, h], mat[pl.ds(begin, width), b * width:(b + 1) * width])
            total = term if total is None else total + term
        return total

    def scatter_copy(h, i, part, sems, landing, landing_sem):
        return pltpu.make_async_remote_copy(
            src_ref=part.at[h, i],
            dst_ref=landing.at[c, h],
            send_sem=sems.at[h, i],
            recv_sem=landing_sem.at[c, h],
            device_id=dev(l, r, far_first(i)),
            device_id_type=MESH,
        )

    def scatter(source, h, mat, part, sems, landing, landing_sem, own):
        for i in range(cols - 1):
            part[h, i] = product(source, h, mat, far_first(i)).astype(jnp.bfloat16)
            scatter_copy(h, i, part, sems, landing, landing_sem).start()
        own[h] = product(source, h, mat, c)

    def arrived(landing, landing_sem, index, h):
        pltpu.make_async_remote_copy(
            src_ref=landing.at[index, h],
            dst_ref=landing.at[index, h],
            send_sem=p1_sem.at[0, 0],
            recv_sem=landing_sem.at[index, h],
            device_id=dev(l, r, lax.rem(c + 1, cols)),
            device_id_type=MESH,
        ).wait_recv()

    def collected(h, own, landing, landing_sem):
        total = own[h]
        for d in range(1, cols):
            sender = lax.rem(c + d, cols)
            arrived(landing, landing_sem, sender, h)
            total = total + landing[sender, h].astype(jnp.float32)
        return total

    def relay_copy(h, d):
        b = lax.rem(r + d, rows)
        return pltpu.make_async_remote_copy(
            src_ref=xbuf.at[b, h],
            dst_ref=xbuf.at[b, h],
            send_sem=relay_sem.at[h, d],
            recv_sem=x_sem.at[b, h],
            device_id=dev(l, partner, c),
            device_id_type=MESH,
        )

    def receives(body):
        if layers == 2:
            body()
        else:
            pl.when((l == 0) | (l == layers - 1))(body)

    @receives
    def _():
        load_t.wait()
        relayout(stage_t, mat_t)

    known(cols - 1)

    @receives
    def _():
        for h in range(parts):
            for d in source_order:
                arrived(xbuf, x_sem, lax.rem(r + d, rows), h)
                relay_copy(h, d).start()
            for d in source_order:
                arrived(xbuf, x_sem, lax.rem(partner + d, rows), h)
            scatter(xbuf, h, mat_t, part1, p1_sem, rs1, rs1_sem, own1)

    load_r.wait()
    relayout(stage_r, mat_r)

    def gather_copy(h, d):
        return pltpu.make_async_remote_copy(
            src_ref=gbuf.at[r, h],
            dst_ref=gbuf.at[r, h],
            send_sem=g_send_sem.at[h, d],
            recv_sem=g_sem.at[r, h],
            device_id=dev(l, lax.rem(r + d, rows), c),
            device_id_type=MESH,
        )

    gather_order = [d for d in order if d > 0]
    for h in range(parts):
        summed[h] = down_v[h * size:(h + 1) * size] + up_v[h * size:(h + 1) * size]

        @receives
        def _():
            summed[h] = summed[h] + collected(h, own1, rs1, rs1_sem)

        gbuf[r, h] = summed[h].astype(jnp.bfloat16)
        for d in gather_order:
            gather_copy(h, d).start()

    for h in range(parts):
        for d in range(1, rows):
            arrived(gbuf, g_sem, lax.rem(r + d, rows), h)
        scatter(gbuf, h, mat_r, part2, p2_sem, rs2, rs2_sem, own2)

    for h in range(parts):
        out_ref[0, h * size:(h + 1) * size] = summed[h] + collected(h, own2, rs2, rs2_sem)

    @pl.when(l == layers - 2)
    def _():
        for copy in source_copies(send_down, down_sem, l + 1):
            copy.wait_send()

    @pl.when(l == 1)
    def _():
        for copy in source_copies(send_up, up_sem, l - 1):
            copy.wait_send()

    for h in range(parts):
        for i in range(cols - 1):
            @receives
            def _():
                scatter_copy(h, i, part1, p1_sem, rs1, rs1_sem).wait_send()

            scatter_copy(h, i, part2, p2_sem, rs2, rs2_sem).wait_send()
        for d in gather_order:
            gather_copy(h, d).wait_send()

        @receives
        def _():
            for d in source_order:
                relay_copy(h, d).wait_send()


def on_device(down_source, up_source, down_transfer, up_transfer, reflection):
    layers, rows, cols = (lax.axis_size(a) for a in ("layer", "row", "col"))
    own_down, own_up = down_source, up_source
    if layers > 2:
        layer = lax.axis_index("layer")
        down_now, up_now = early_rounds(
            own_down[0], own_up[0], down_transfer, up_transfer, layers - 2
        )
        own_down = jnp.where(layer == layers - 1, own_down, down_now[None])
        own_up = jnp.where(layer == 0, own_up, up_now[None])

    _, sources, width = down_source.shape
    _, height, blocks, piece = down_transfer.shape
    lane = 128
    halves = piece // lane
    groups = halves * blocks

    def tiles(w):
        return w.reshape(height, blocks, halves, lane).transpose(0, 2, 1, 3).reshape(-1, lane)

    parts = PARTS
    size = sources // parts
    any_space = pl.BlockSpec(memory_space=pl.ANY)
    vmem = pltpu.VMEM
    f32, bf16 = jnp.float32, jnp.bfloat16
    dma = pltpu.SemaphoreType.DMA
    step = min(height, 256)
    return pl.pallas_call(
        functools.partial(kernel, layers, rows, cols),
        out_shape=pltpu.VMEM(down_source.shape, f32),
        in_specs=[any_space] * 5,
        out_specs=pl.BlockSpec(memory_space=pltpu.VMEM),
        scratch_shapes=[
            vmem((sources, width), f32),
            vmem((sources, width), f32),
            vmem((height * groups, lane), bf16),
            vmem((height * groups, lane), bf16),
            vmem((step * groups, lane), f32),
            vmem((height, blocks * piece), bf16),
            vmem((height, blocks * piece), bf16),
            vmem((parts, size, width), bf16),
            vmem((parts, size, width), bf16),
            vmem((rows, parts, size, width), bf16),
            vmem((parts, cols - 1, size, width), bf16),
            vmem((cols, parts, size, width), bf16),
            vmem((parts, size, width), f32),
            vmem((parts, size, width), f32),
            vmem((rows, parts, size, width), bf16),
            vmem((parts, cols - 1, size, width), bf16),
            vmem((cols, parts, size, width), bf16),
            vmem((parts, size, width), f32),
            dma((4,)),
            dma((parts, rows)),
            dma((parts, rows)),
            dma((rows, parts)),
            dma((parts, cols - 1)),
            dma((cols, parts)),
            dma((parts, rows)),
            dma((rows, parts)),
            dma((parts, cols - 1)),
            dma((cols, parts)),
            dma((parts, rows)),
            pltpu.SemaphoreType.REGULAR((2, cols)),
        ],
        compiler_params=pltpu.CompilerParams(collective_id=0, has_side_effects=True),
    )(own_down, own_up, tiles(down_transfer), tiles(up_transfer), tiles(reflection))


def solution(mesh):
    in_specs = (
        P("layer", None, ("row", "col")),
        P("layer", None, ("row", "col")),
        P("layer", "row", None, "col"),
        P("layer", "row", None, "col"),
        P("layer", "row", None, "col"),
    )
    out_specs = P("layer", None, ("row", "col"))
    return jax.shard_map(
        on_device, mesh=mesh, in_specs=in_specs, out_specs=out_specs, check_vma=False
    )
```

```python
import functools

import jax
import jax.numpy as jnp
from jax import lax
from jax.experimental import pallas as pl
from jax.experimental.pallas import tpu as pltpu
from jax.sharding import PartitionSpec as P

EARLY = 1
ORD = 0
PARTS = 1
MESH = pl.DeviceIdType.MESH


def passed_along(block, axis, distance):
    devices = range(lax.axis_size(axis))
    route = [(i - distance, i) for i in devices if i - distance in devices]
    return lax.ppermute(block, axis, route)


def contract(data_rows, matrix_rows):
    return lax.dot_general(
        data_rows, matrix_rows, (((1,), (1,)), ((), ())), preferred_element_type=jnp.float32
    )


def early_rounds(own_down, own_up, down_transfer, up_transfer, rounds):
    height = down_transfer.shape[1]
    down_tile = down_transfer[0].reshape(height, -1)
    up_tile = up_transfer[0].reshape(height, -1)

    def gain(trace, distance, tile):
        moved = passed_along(trace.astype(jnp.bfloat16), "layer", distance)
        pieces = lax.all_gather(moved, "row", axis=1, tiled=True)
        return lax.psum_scatter(contract(pieces, tile), "col", scatter_dimension=1, tiled=True)

    def one(counter, carried):
        down_now, up_now = carried
        return own_down + gain(down_now, 1, down_tile), own_up + gain(up_now, -1, up_tile)

    return lax.fori_loop(0, rounds, one, (own_down, own_up))


def kernel(
    layers, rows, cols,
    down_ref, up_ref, wdown_ref, wup_ref, wreflect_ref, out_ref,
    down_v, up_v, stage_t, stage_r, wide, mat_t, mat_r,
    send_down, send_up, xbuf, part1, rs1, own1, summed, gbuf, part2, rs2, own2,
    load_sem, down_sem, up_sem, x_sem, p1_sem, rs1_sem, g_send_sem, g_sem, p2_sem, rs2_sem,
    early, relay_sem, far_sem,
):
    l, r, c = lax.axis_index("layer"), lax.axis_index("row"), lax.axis_index("col")
    parts, size, width = xbuf.shape[1:]
    groups = stage_t.shape[0] // mat_t.shape[0]
    lane = stage_t.shape[1]

    def dev(layer, row, col):
        return (layer, row, col)

    order = sorted(range(rows), key=lambda d: (abs(d - rows // 2), -d))
    partner = r + 1 - 2 * lax.rem(r, 2)

    barrier = pltpu.get_barrier_semaphore()

    def greet(layer, row, col):
        pl.semaphore_signal(barrier, inc=1, device_id=dev(layer, row, col), device_id_type=MESH)

    source_order = [d for d in order if d % 2 == 0]
    if layers == 2:
        for d in source_order:
            greet(1 - l, lax.rem(r + d, rows), c)
        neighbours = 1
    else:
        @pl.when(l > 0)
        def _():
            for d in source_order:
                greet(l - 1, lax.rem(r + d, rows), c)

        @pl.when(l < layers - 1)
        def _():
            for d in source_order:
                greet(l + 1, lax.rem(r + d, rows), c)

        neighbours = jnp.where(l > 0, 1, 0) + jnp.where(l < layers - 1, 1, 0)

    @pl.when(c > 0)
    def _():
        greet(l, r, c - 1)

    @pl.when(c < cols - 1)
    def _():
        greet(l, r, c + 1)

    beside = jnp.where(c > 0, 1, 0) + jnp.where(c < cols - 1, 1, 0)
    for d in range(1, rows):
        greet(l, lax.rem(r + d, rows), c)

    load_down = pltpu.make_async_copy(down_ref.at[0], down_v, load_sem.at[0])
    load_up = pltpu.make_async_copy(up_ref.at[0], up_v, load_sem.at[1])
    load_down.start()
    load_up.start()
    load_t = pltpu.make_async_copy(wdown_ref, stage_t, load_sem.at[2])
    load_tu = pltpu.make_async_copy(wup_ref, stage_t, load_sem.at[2])
    load_r = pltpu.make_async_copy(wreflect_ref, stage_r, load_sem.at[3])

    @pl.when(l == 0)
    def _():
        load_tu.start()

    @pl.when(l == layers - 1)
    def _():
        load_t.start()

    load_r.start()

    load_down.wait()
    load_up.wait()
    for h in range(parts):
        send_down[h] = down_v[h * size:(h + 1) * size].astype(jnp.bfloat16)
        send_up[h] = up_v[h * size:(h + 1) * size].astype(jnp.bfloat16)
    pl.semaphore_wait(barrier, len(source_order) * neighbours + (rows - 1) + beside)

    def source_copies(buffer, sems, layer):
        return [
            pltpu.make_async_remote_copy(
                src_ref=buffer.at[h],
                dst_ref=xbuf.at[r, h],
                send_sem=sems.at[h, d],
                recv_sem=x_sem.at[r, h],
                device_id=dev(layer, lax.rem(r + d, rows), c),
                device_id_type=MESH,
            )
            for h in range(parts)
            for d in source_order
        ]

    @pl.when(l == layers - 2)
    def _():
        for copy in source_copies(send_down, down_sem, l + 1):
            copy.start()

    @pl.when(l == 1)
    def _():
        for copy in source_copies(send_up, up_sem, l - 1):
            copy.start()

    def tell(hop, side, col):
        pl.semaphore_signal(
            far_sem.at[side, hop], inc=1, device_id=dev(l, r, col), device_id_type=MESH
        )

    def known(hop):
        for side, sign in ((0, -1), (1, 1)):
            there = (c >= hop) if sign < 0 else (c < cols - hop)
            onward = (c < cols - 1) if sign < 0 else (c > 0)

            if hop > 1:
                @pl.when(there)
                def _():
                    pl.semaphore_wait(far_sem.at[side, hop], 1)

            if hop < cols - 1:
                @pl.when(there & onward)
                def _():
                    tell(hop + 1, side, c - sign)

    for hop in range(1, cols - 1):
        known(hop)

    def relayout(stage, mat):
        step = wide.shape[0] // groups

        def one(i, carry):
            wide[...] = stage[pl.ds(pl.multiple_of(i * step * groups, 128), step * groups), :].astype(jnp.float32)
            blocks = groups * lane // width
            for g in range(groups):
                half, b = divmod(g, blocks)
                column = b * width + half * lane
                mat[pl.ds(pl.multiple_of(i * step, 128), step), column:column + lane] = wide[
                    pl.ds(g, step, stride=groups), :
                ].astype(jnp.bfloat16)
            return carry

        lax.fori_loop(0, mat.shape[0] // step, one, 0)

    def far_first(i):
        if ORD == 1:
            i = cols - 2 - i
        if ORD == 2:
            return lax.rem(c + 2 + i, cols) if i < 2 else lax.rem(c + 1, cols)
        low = 2 * c < cols - 1
        down_t = cols - 1 - i
        down_t = jnp.where(down_t <= c, down_t - 1, down_t)
        up_t = jnp.where(c <= i, i + 1, i)
        return jnp.where(low, down_t, up_t)

    def product(source, h, mat, target, blocks):
        begin = pl.multiple_of(target * width, 128)
        total = None
        for b in blocks:
            column = b * width if isinstance(b, int) else pl.multiple_of(b * width, 128)
            term = contract(source[b, h], mat[pl.ds(begin, width), pl.ds(column, width)])
            total = term if total is None else total + term
        return total

    def scatter_copy(h, i, part, sems, landing, landing_sem):
        return pltpu.make_async_remote_copy(
            src_ref=part.at[h, i],
            dst_ref=landing.at[c, h],
            send_sem=sems.at[h, i],
            recv_sem=landing_sem.at[c, h],
            device_id=dev(l, r, far_first(i)),
            device_id_type=MESH,
        )

    def scatter(source, source_sem, first, rest, h, mat, part, sems, landing, landing_sem, own):
        targets = [far_first(i) for i in range(cols - 1)] + [c]
        if first:
            for i, target in enumerate(targets):
                early[i] = product(source, h, mat, target, first)
        for b in rest:
            arrived(source, source_sem, b, h)
        for i, target in enumerate(targets):
            if first:
                total = early[i] + product(source, h, mat, target, rest)
            else:
                total = product(source, h, mat, target, range(rows))
            if i < cols - 1:
                part[h, i] = total.astype(jnp.bfloat16)
                scatter_copy(h, i, part, sems, landing, landing_sem).start()
            else:
                own[h] = total

    def arrived(landing, landing_sem, index, h):
        pltpu.make_async_remote_copy(
            src_ref=landing.at[index, h],
            dst_ref=landing.at[index, h],
            send_sem=p1_sem.at[0, 0],
            recv_sem=landing_sem.at[index, h],
            device_id=dev(l, r, lax.rem(c + 1, cols)),
            device_id_type=MESH,
        ).wait_recv()

    def collected(h, own, landing, landing_sem):
        total = own[h]
        for d in range(1, cols):
            sender = lax.rem(c + d, cols)
            arrived(landing, landing_sem, sender, h)
            total = total + landing[sender, h].astype(jnp.float32)
        return total

    def relay_copy(h, d):
        b = lax.rem(r + d, rows)
        return pltpu.make_async_remote_copy(
            src_ref=xbuf.at[b, h],
            dst_ref=xbuf.at[b, h],
            send_sem=relay_sem.at[h, d],
            recv_sem=x_sem.at[b, h],
            device_id=dev(l, partner, c),
            device_id_type=MESH,
        )

    def receives(body):
        if layers == 2:
            body()
        else:
            pl.when((l == 0) | (l == layers - 1))(body)

    @receives
    def _():
        load_t.wait()
        relayout(stage_t, mat_t)

    known(cols - 1)

    @receives
    def _():
        for h in range(parts):
            for d in source_order:
                arrived(xbuf, x_sem, lax.rem(r + d, rows), h)
                relay_copy(h, d).start()
            rest = [lax.rem(partner + d, rows) for d in source_order]
            first = [lax.rem(r + d, rows) for d in source_order]
            scatter(xbuf, x_sem, first if EARLY > 1 else [], rest, h, mat_t, part1, p1_sem, rs1, rs1_sem, own1)

    load_r.wait()
    relayout(stage_r, mat_r)

    def gather_copy(h, d):
        return pltpu.make_async_remote_copy(
            src_ref=gbuf.at[r, h],
            dst_ref=gbuf.at[r, h],
            send_sem=g_send_sem.at[h, d],
            recv_sem=g_sem.at[r, h],
            device_id=dev(l, lax.rem(r + d, rows), c),
            device_id_type=MESH,
        )

    gather_order = [d for d in order if d > 0]
    for h in range(parts):
        summed[h] = down_v[h * size:(h + 1) * size] + up_v[h * size:(h + 1) * size]

        @receives
        def _():
            summed[h] = summed[h] + collected(h, own1, rs1, rs1_sem)

        gbuf[r, h] = summed[h].astype(jnp.bfloat16)
        for d in gather_order:
            gather_copy(h, d).start()

    for h in range(parts):
        if EARLY:
            arrived(gbuf, g_sem, partner, h)
            first = [r, partner]
            rest = [lax.rem(r - lax.rem(r, 2) + d, rows) for d in range(2, rows)]
        else:
            first = []
            rest = [lax.rem(r + d, rows) for d in range(1, rows)]
        scatter(gbuf, g_sem, first, rest, h, mat_r, part2, p2_sem, rs2, rs2_sem, own2)

    for h in range(parts):
        out_ref[0, h * size:(h + 1) * size] = summed[h] + collected(h, own2, rs2, rs2_sem)

    @pl.when(l == layers - 2)
    def _():
        for copy in source_copies(send_down, down_sem, l + 1):
            copy.wait_send()

    @pl.when(l == 1)
    def _():
        for copy in source_copies(send_up, up_sem, l - 1):
            copy.wait_send()

    for h in range(parts):
        for i in range(cols - 1):
            @receives
            def _():
                scatter_copy(h, i, part1, p1_sem, rs1, rs1_sem).wait_send()

            scatter_copy(h, i, part2, p2_sem, rs2, rs2_sem).wait_send()
        for d in gather_order:
            gather_copy(h, d).wait_send()

        @receives
        def _():
            for d in source_order:
                relay_copy(h, d).wait_send()


def on_device(down_source, up_source, down_transfer, up_transfer, reflection):
    layers, rows, cols = (lax.axis_size(a) for a in ("layer", "row", "col"))
    own_down, own_up = down_source, up_source
    if layers > 2:
        layer = lax.axis_index("layer")
        down_now, up_now = early_rounds(
            own_down[0], own_up[0], down_transfer, up_transfer, layers - 2
        )
        own_down = jnp.where(layer == layers - 1, own_down, down_now[None])
        own_up = jnp.where(layer == 0, own_up, up_now[None])

    _, sources, width = down_source.shape
    _, height, blocks, piece = down_transfer.shape
    lane = 128
    halves = piece // lane
    groups = halves * blocks

    def tiles(w):
        return w.reshape(height, blocks, halves, lane).transpose(0, 2, 1, 3).reshape(-1, lane)

    parts = PARTS
    size = sources // parts
    any_space = pl.BlockSpec(memory_space=pl.ANY)
    vmem = pltpu.VMEM
    f32, bf16 = jnp.float32, jnp.bfloat16
    dma = pltpu.SemaphoreType.DMA
    step = min(height, 256)
    return pl.pallas_call(
        functools.partial(kernel, layers, rows, cols),
        out_shape=pltpu.VMEM(down_source.shape, f32),
        in_specs=[any_space] * 5,
        out_specs=pl.BlockSpec(memory_space=pltpu.VMEM),
        scratch_shapes=[
            vmem((sources, width), f32),
            vmem((sources, width), f32),
            vmem((height * groups, lane), bf16),
            vmem((height * groups, lane), bf16),
            vmem((step * groups, lane), f32),
            vmem((height, blocks * piece), bf16),
            vmem((height, blocks * piece), bf16),
            vmem((parts, size, width), bf16),
            vmem((parts, size, width), bf16),
            vmem((rows, parts, size, width), bf16),
            vmem((parts, cols - 1, size, width), bf16),
            vmem((cols, parts, size, width), bf16),
            vmem((parts, size, width), f32),
            vmem((parts, size, width), f32),
            vmem((rows, parts, size, width), bf16),
            vmem((parts, cols - 1, size, width), bf16),
            vmem((cols, parts, size, width), bf16),
            vmem((parts, size, width), f32),
            dma((4,)),
            dma((parts, rows)),
            dma((parts, rows)),
            dma((rows, parts)),
            dma((parts, cols - 1)),
            dma((cols, parts)),
            dma((parts, rows)),
            dma((rows, parts)),
            dma((parts, cols - 1)),
            dma((cols, parts)),
            vmem((cols, size, width), f32),
            dma((parts, rows)),
            pltpu.SemaphoreType.REGULAR((2, cols)),
        ],
        compiler_params=pltpu.CompilerParams(collective_id=0, has_side_effects=True),
    )(own_down, own_up, tiles(down_transfer), tiles(up_transfer), tiles(reflection))


def solution(mesh):
    in_specs = (
        P("layer", None, ("row", "col")),
        P("layer", None, ("row", "col")),
        P("layer", "row", None, "col"),
        P("layer", "row", None, "col"),
        P("layer", "row", None, "col"),
    )
    out_specs = P("layer", None, ("row", "col"))
    return jax.shard_map(
        on_device, mesh=mesh, in_specs=in_specs, out_specs=out_specs, check_vma=False
    )
```
